32 devices in a mesh: rep: 2 (over y), fsdp: 4 (over z), section: 4 (over x, core).
Axes of the slice: x: 2, y: 2, z: 4, core: 2. Of those that a mesh axis runs over, the one named last changes fastest.
Arguments:
- iterate: bfloat16 [8, 3072, 1024], P(('rep', 'section'), None, 'fsdp'), parts along dimension 0, may hold values from -0.1875 to 0.1875
Outputs:
- update: bfloat16 [8, 3072, 1024], P(('rep', 'section'), None, 'fsdp'), parts along dimension 0
The draws below stay inside these ranges and needn't reach their ends.
There are 2 independent parts, one for each index of `rep`. The reference program is written for one: setup_inputs(seed, part) draws one part's arguments, and reference() takes and returns one part's arrays. A program takes and returns all parts, laid end to end along the dimension named above; each array names one. Nothing has to cross between parts.
All inputs are finite; a program needn't handle non-finite values.
Results may differ from the reference program's by a relative error of at most 0.0055.
Values may be sent and summed in bfloat16 or wider, within the bound.
A program may use at most 128 MiB of HBM per device.

```python
import math
import jax
import jax.numpy as jnp
from jax import lax

D = 3072
COLS_DEV = 256
COLS = 1024
EXPERTS = 4
N_FSDP = 4


def block_levels(rng, dims, cuts, least, high):
    def one(position, parts):
        draws = jax.random.uniform(jax.random.fold_in(jax.random.fold_in(rng, 6), position), (parts,), jnp.float32, least / len(cuts), high / len(cuts))
        return jnp.repeat(jnp.exp(draws), dims[position] // parts).reshape((-1,) + (1,) * (len(dims) - position - 1))

    level = one(*cuts[0])
    for cut in cuts[1:]:
        level = level * one(*cut)
    return level


def scatter_about(own_key, shape, scale, most, split=(), held_as=jnp.bfloat16):
    drawn = jax.random.normal(own_key, shape, jnp.float32) * scale
    if len(split) > 0:
        drawn = block_levels(own_key, shape, split, -0.22, 0.18) * drawn
    return jnp.clip(drawn, min=-most, max=most).astype(held_as)


def setup_inputs(seed: int = 0, part: int = 0) -> dict:
    arg_keys = jax.random.split(jax.random.key(seed), 2)
    own_keys = jax.random.split(jax.random.fold_in(arg_keys[1], part), 2)
    return {
        "iterate": scatter_about(own_keys[0], (EXPERTS, D, COLS), (1.1 / (COLS ** 0.5 + D ** 0.5)), 0.1875, ((0, 4), (2, 4))),
    }


def reference(iterate):
    results = []
    out_scale = 0.2 * math.sqrt(max(D, COLS))
    for expert in range(EXPERTS):
        expert_rows = iterate[expert]

        def add_block(index, total):
            block = lax.dynamic_slice_in_dim(expert_rows, (index * COLS_DEV).astype(jnp.int32), COLS_DEV, 1)
            part = jnp.dot(block, block.T, preferred_element_type=jnp.float32).astype(jnp.bfloat16)
            return total + part.astype(jnp.float32)
        gram_sum = lax.fori_loop(jnp.int32(0), jnp.int32(N_FSDP), add_block, jnp.zeros((D, D), jnp.float32))
        gram_half = gram_sum.astype(jnp.bfloat16)
        first_product = jnp.dot(gram_half, expert_rows, preferred_element_type=jnp.float32)
        first_half = first_product.astype(jnp.bfloat16)
        second_product = jnp.dot(gram_half, first_half, preferred_element_type=jnp.float32)
        combined = out_scale * (3.4445 * expert_rows.astype(jnp.float32) - 4.775 * first_product + 2.0315 * second_product)
        results.append(combined.astype(jnp.bfloat16))
    return jnp.stack(results)
```

```python
import math

import jax
import jax.numpy as jnp
import numpy as np
from jax import lax
from jax.sharding import PartitionSpec as P


def tile_table(devices, band_blocks):
    block_table = np.zeros((devices, devices), dtype=np.int32)
    for row_block in range(devices):
        for col_block in range(devices):
            distance = (col_block - row_block) % devices
            if distance <= devices // 2:
                block_table[row_block, col_block] = row_block * band_blocks + distance
            else:
                block_table[row_block, col_block] = (
                    devices * band_blocks + col_block * band_blocks + (devices - distance)
                )
    return block_table


def on_device(iterate):
    devices = lax.axis_size("fsdp")
    experts, rows_all, columns = iterate.shape
    strip_rows = rows_all // devices
    band_blocks = devices // 2 + 1
    out_scale = 0.2 * math.sqrt(max(rows_all, columns * devices))
    expert_rows = iterate[0]
    row_blocks = expert_rows.reshape(devices, strip_rows, columns)

    def one_offset(offset):
        partner = jnp.roll(row_blocks, -offset, axis=0)
        tiles = jnp.einsum("nsc,ntc->nst", row_blocks, partner, preferred_element_type=jnp.float32)
        return tiles.astype(jnp.bfloat16)

    band_term = lax.map(one_offset, jnp.arange(band_blocks, dtype=jnp.int32))
    received = lax.all_to_all(band_term, "fsdp", split_axis=1, concat_axis=1, tiled=True)
    own_band = jnp.sum(received.astype(jnp.float32), axis=1).astype(jnp.bfloat16)
    upper_tiles = lax.all_gather(own_band, "fsdp", axis=0, tiled=True)
    tile_pool = jnp.concatenate([upper_tiles, jnp.swapaxes(upper_tiles, 1, 2)], axis=0)
    block_table = jnp.asarray(tile_table(devices, band_blocks))
    dense_blocks = jnp.take(tile_pool, block_table, axis=0)

    def apply_gram(operand):
        shaped = operand.reshape(devices, strip_rows, columns)
        product = jnp.einsum(
            "nmij,mjc->nic", dense_blocks, shaped, preferred_element_type=jnp.float32
        )
        return product.reshape(rows_all, columns)

    first_product = apply_gram(expert_rows)
    second_product = apply_gram(first_product.astype(jnp.bfloat16))
    combined = out_scale * (
        3.4445 * expert_rows.astype(jnp.float32) - 4.775 * first_product + 2.0315 * second_product
    )
    results = [combined.astype(jnp.bfloat16)]
    return jnp.stack(results)


def on_device_columns(iterate):
    devices = lax.axis_size("fsdp")
    own = lax.axis_index("fsdp")
    _, rows_all, columns = iterate.shape
    out_scale = 0.2 * math.sqrt(max(rows_all, columns * devices))
    gathered = lax.all_gather(iterate[0], "fsdp", axis=1, tiled=True)
    gram = lax.dot_general(
        gathered, gathered, (((0,), (0,)), ((), ())), preferred_element_type=jnp.float32
    )
    gram_half = gram.astype(jnp.bfloat16)
    own_gram = lax.dynamic_slice_in_dim(gram, own * columns, columns, 1)
    square = jnp.dot(gram_half, own_gram.astype(jnp.bfloat16), preferred_element_type=jnp.float32)
    row_ids = lax.broadcasted_iota(jnp.int32, square.shape, 0)
    column_ids = lax.broadcasted_iota(jnp.int32, square.shape, 1) + own * columns
    identity = (row_ids == column_ids).astype(jnp.float32)
    mixing = out_scale * (3.4445 * identity - 4.775 * own_gram + 2.0315 * square)
    update = jnp.dot(gathered, mixing.astype(jnp.bfloat16), preferred_element_type=jnp.float32)
    return update.astype(jnp.bfloat16)[None]


def for_shapes(iterate):
    _, rows_all, columns = iterate.shape
    if columns * lax.axis_size("fsdp") <= rows_all:
        return on_device_columns(iterate)
    return on_device(iterate)


def solution(mesh):
    return jax.shard_map(
        for_shapes,
        mesh=mesh,
        in_specs=(P(("rep", "section"), None, "fsdp"),),
        out_specs=P(("rep", "section"), None, "fsdp"),
        check_vma=False,
    )
```

```python
import functools
import math

import jax
import jax.numpy as jnp
import numpy as np
from jax import lax
from jax.experimental import pallas as pl
from jax.experimental.pallas import tpu as pltpu
from jax.sharding import PartitionSpec as P


def tile_table(devices, band_blocks):
    block_table = np.zeros((devices, devices), dtype=np.int32)
    for row_block in range(devices):
        for col_block in range(devices):
            distance = (col_block - row_block) % devices
            if distance <= devices // 2:
                block_table[row_block, col_block] = row_block * band_blocks + distance
            else:
                block_table[row_block, col_block] = (
                    devices * band_blocks + col_block * band_blocks + (devices - distance)
                )
    return block_table


def on_device(iterate):
    devices = lax.axis_size("fsdp")
    experts, rows_all, columns = iterate.shape
    strip_rows = rows_all // devices
    band_blocks = devices // 2 + 1
    out_scale = 0.2 * math.sqrt(max(rows_all, columns * devices))
    expert_rows = iterate[0]
    row_blocks = expert_rows.reshape(devices, strip_rows, columns)

    def one_offset(offset):
        partner = jnp.roll(row_blocks, -offset, axis=0)
        tiles = jnp.einsum("nsc,ntc->nst", row_blocks, partner, preferred_element_type=jnp.float32)
        return tiles.astype(jnp.bfloat16)

    band_term = lax.map(one_offset, jnp.arange(band_blocks, dtype=jnp.int32))
    received = lax.all_to_all(band_term, "fsdp", split_axis=1, concat_axis=1, tiled=True)
    own_band = jnp.sum(received.astype(jnp.float32), axis=1).astype(jnp.bfloat16)
    upper_tiles = lax.all_gather(own_band, "fsdp", axis=0, tiled=True)
    tile_pool = jnp.concatenate([upper_tiles, jnp.swapaxes(upper_tiles, 1, 2)], axis=0)
    block_table = jnp.asarray(tile_table(devices, band_blocks))
    dense_blocks = jnp.take(tile_pool, block_table, axis=0)

    def apply_gram(operand):
        shaped = operand.reshape(devices, strip_rows, columns)
        product = jnp.einsum(
            "nmij,mjc->nic", dense_blocks, shaped, preferred_element_type=jnp.float32
        )
        return product.reshape(rows_all, columns)

    first_product = apply_gram(expert_rows)
    second_product = apply_gram(first_product.astype(jnp.bfloat16))
    combined = out_scale * (
        3.4445 * expert_rows.astype(jnp.float32) - 4.775 * first_product + 2.0315 * second_product
    )
    results = [combined.astype(jnp.bfloat16)]
    return jnp.stack(results)


CHUNK = 128
GROUP = 2
EXTRA = 0
SHIFT = 4.775 / (2 * 2.0315)
BASE = 3.4445 - 4.775 * 4.775 / (4 * 2.0315)


def line_kernel(
    out_scale, chunks, direct,
    x_ref, out_ref,
    xall, gram, half, mixing, staged, sent_rows,
    local_sem, store_sem, recv_sem, inner_sem, outer_sem, mix_send, mix_recv, row_send, row_recv,
):
    me = lax.axis_index("fsdp")
    columns = x_ref.shape[1]
    width = columns * 4
    span = CHUNK * GROUP
    middle = jnp.logical_and(me > 0, me < 3)
    end = jnp.logical_not(middle)

    def rows_of(k):
        return pl.ds(pl.multiple_of(k * CHUNK, CHUNK), CHUNK)

    own_copy = pltpu.make_async_copy(x_ref, xall.at[me], local_sem)
    own_copy.start()

    barrier = pltpu.get_barrier_semaphore()

    @pl.when(me > 0)
    def _():
        pl.semaphore_signal(barrier, inc=1, device_id={"fsdp": me - 1}, device_id_type=pl.DeviceIdType.MESH)

    @pl.when(me < 3)
    def _():
        pl.semaphore_signal(barrier, inc=1, device_id={"fsdp": me + 1}, device_id_type=pl.DeviceIdType.MESH)

    @pl.when(middle)
    def _():
        pl.semaphore_wait(barrier, 2)

    @pl.when(end)
    def _():
        pl.semaphore_wait(barrier, 1)

    def own_chunk(k, sem, target):
        return pltpu.make_async_remote_copy(
            src_ref=x_ref.at[rows_of(k)], dst_ref=xall.at[me, rows_of(k)],
            send_sem=sem, recv_sem=recv_sem.at[me, k],
            device_id={"fsdp": target}, device_id_type=pl.DeviceIdType.MESH,
        )

    def relay_chunk(shard, k, sem, target):
        return pltpu.make_async_remote_copy(
            src_ref=xall.at[shard, rows_of(k)], dst_ref=xall.at[shard, rows_of(k)],
            send_sem=sem, recv_sem=recv_sem.at[shard, k],
            device_id={"fsdp": target}, device_id_type=pl.DeviceIdType.MESH,
        )

    def mix_copy(target):
        return pltpu.make_async_remote_copy(
            src_ref=mixing.at[0], dst_ref=mixing.at[0],
            send_sem=mix_send, recv_sem=mix_recv,
            device_id={"fsdp": target}, device_id_type=pl.DeviceIdType.MESH,
        )

    def row_copy(k, target):
        return pltpu.make_async_remote_copy(
            src_ref=sent_rows.at[pl.ds(pl.multiple_of((k - direct) * CHUNK, CHUNK), CHUNK)],
            dst_ref=out_ref.at[rows_of(k)],
            send_sem=row_send.at[k], recv_sem=row_recv.at[k],
            device_id={"fsdp": target}, device_id_type=pl.DeviceIdType.MESH,
        )

    def wide(rows):
        return jnp.concatenate([xall[q, rows, :] for q in range(4)], axis=1)

    def update_rows(shard, slot, rows):
        product = jnp.dot(wide(rows), mixing[slot], preferred_element_type=jnp.float32)
        own = xall[shard, rows, :].astype(jnp.float32)
        return (out_scale * BASE * own + product).astype(jnp.bfloat16)

    def store_copy(k):
        return pltpu.make_async_copy(staged.at[rows_of(k)], out_ref.at[rows_of(k)], store_sem.at[k])

    @pl.when(middle)
    def _():
        peer = 3 - me
        outer = 3 * (me - 1)
        far = 3 - outer

        @pl.loop(0, chunks)
        def _(k):
            own_chunk(k, inner_sem.at[0, k], peer).start()

            @pl.when(k < direct)
            def _():
                own_chunk(k, outer_sem.at[0, k], outer).start()

        for i in range(4):
            row_ids = lax.broadcasted_iota(jnp.int32, (columns, width), 0) + i * columns
            column_ids = lax.broadcasted_iota(jnp.int32, (columns, width), 1)
            gram[i] = jnp.where(row_ids == column_ids, jnp.float32(-SHIFT), jnp.float32(0))
        own_copy.wait()

        @pl.loop(0, chunks)
        def _(k):
            relay_chunk(outer, k, inner_sem.at[1, k], peer).wait_recv()
            relay_chunk(outer, k, inner_sem.at[1, k], peer).start()
            relay_chunk(peer, k, outer_sem.at[1, k], outer).wait_recv()

            @pl.when(k < direct)
            def _():
                relay_chunk(peer, k, outer_sem.at[1, k], outer).start()

        def take_far(k):
            relay_chunk(far, k, outer_sem.at[2, k], outer).wait_recv()

            @pl.when(k < direct)
            def _():
                relay_chunk(far, k, outer_sem.at[2, k], outer).start()

        def partial(step, i):
            rows = pl.ds(pl.multiple_of(step * span, span), span)
            return lax.dot_general(
                xall[i, rows, :], wide(rows), (((0,), (0,)), ((), ())),
                preferred_element_type=jnp.float32,
            )

        steps = chunks // GROUP

        @pl.loop(0, steps - 1)
        def _(step):
            for g in range(GROUP):
                take_far(step * GROUP + g)
            for i in range(4):
                gram[i] += partial(step, i)

        for g in range(GROUP):
            take_far((steps - 1) * GROUP + g)
        for i in range(4):
            total = (gram[i] + partial(steps - 1, i)).astype(jnp.bfloat16)
            for j in range(4):
                half[j, i * columns:(i + 1) * columns, :] = total[:, j * columns:(j + 1) * columns]

        def mix(slot, shard):
            for i in range(4):
                left = jnp.concatenate(
                    [half[j, i * columns:(i + 1) * columns, :] for j in range(4)], axis=1
                )
                square = jnp.dot(left, half[shard], preferred_element_type=jnp.float32)
                mixing[slot, i * columns:(i + 1) * columns, :] = (
                    (out_scale * 2.0315) * square
                ).astype(jnp.bfloat16)

        mix(0, outer)
        mix_copy(outer).start()

        @pl.loop(direct, chunks)
        def _(k):
            sent_rows[pl.ds(pl.multiple_of((k - direct) * CHUNK, CHUNK), CHUNK), :] = update_rows(
                outer, 0, rows_of(k)
            )
            row_copy(k, outer).start()

        mix(1, me)

        @pl.loop(0, chunks)
        def _(k):
            staged[rows_of(k), :] = update_rows(me, 1, rows_of(k))
            store_copy(k).start()

        @pl.loop(0, chunks)
        def _(k):
            store_copy(k).wait()
            own_chunk(k, inner_sem.at[0, k], peer).wait_send()
            relay_chunk(outer, k, inner_sem.at[1, k], peer).wait_send()

        @pl.loop(0, direct)
        def _(k):
            own_chunk(k, outer_sem.at[0, k], outer).wait_send()
            relay_chunk(peer, k, outer_sem.at[1, k], outer).wait_send()
            relay_chunk(far, k, outer_sem.at[2, k], outer).wait_send()

        mix_copy(outer).wait_send()

        @pl.loop(direct, chunks)
        def _(k):
            row_copy(k, outer).wait_send()

    @pl.when(end)
    def _():
        inner = 1 + me // 3

        @pl.loop(0, chunks)
        def _(k):
            own_chunk(k, inner_sem.at[0, k], inner).start()

        own_copy.wait()
        for hop in range(3):
            shard = inner + hop * (1 - 2 * (me // 3))

            @pl.loop(0, direct)
            def _(k):
                relay_chunk(shard, k, outer_sem.at[0, k], inner).wait_recv()

        mix_copy(inner).wait_recv()

        @pl.loop(0, direct)
        def _(k):
            staged[rows_of(k), :] = update_rows(me, 0, rows_of(k))
            store_copy(k).start()

        @pl.loop(0, direct)
        def _(k):
            store_copy(k).wait()

        @pl.loop(0, chunks)
        def _(k):
            own_chunk(k, inner_sem.at[0, k], inner).wait_send()

        @pl.loop(direct, chunks)
        def _(k):
            row_copy(k, inner).wait_recv()


def on_device_line(iterate):
    _, rows_all, columns = iterate.shape
    width = columns * 4
    chunks = rows_all // CHUNK
    direct = 2 * chunks // 3 + EXTRA
    out_scale = 0.2 * math.sqrt(max(rows_all, width))
    update = pl.pallas_call(
        functools.partial(line_kernel, out_scale, chunks, direct),
        out_shape=jax.ShapeDtypeStruct((rows_all, columns), jnp.bfloat16),
        in_specs=[pl.BlockSpec(memory_space=pl.ANY)],
        out_specs=pl.BlockSpec(memory_space=pl.ANY),
        scratch_shapes=[
            pltpu.VMEM((4, rows_all, columns), jnp.bfloat16),
            pltpu.VMEM((4, columns, width), jnp.float32),
            pltpu.VMEM((4, width, columns), jnp.bfloat16),
            pltpu.VMEM((2, width, columns), jnp.bfloat16),
            pltpu.VMEM((rows_all, columns), jnp.bfloat16),
            pltpu.VMEM(((chunks - direct) * CHUNK, columns), jnp.bfloat16),
            pltpu.SemaphoreType.DMA,
            pltpu.SemaphoreType.DMA((chunks,)),
            pltpu.SemaphoreType.DMA((4, chunks)),
            pltpu.SemaphoreType.DMA((2, chunks)),
            pltpu.SemaphoreType.DMA((3, chunks)),
            pltpu.SemaphoreType.DMA,
            pltpu.SemaphoreType.DMA,
            pltpu.SemaphoreType.DMA((chunks,)),
            pltpu.SemaphoreType.DMA((chunks,)),
        ],
        compiler_params=pltpu.CompilerParams(
            collective_id=0, has_side_effects=True, vmem_limit_bytes=56 << 20
        ),
    )(iterate[0])
    return update[None]


def for_shapes(iterate):
    _, rows_all, columns = iterate.shape
    devices = lax.axis_size("fsdp")
    fits = columns % 256 == 0 and rows_all % (3 * CHUNK * GROUP) == 0
    if devices == 4 and columns * devices <= rows_all and fits:
        return on_device_line(iterate)
    return on_device(iterate)


def solution(mesh):
    return jax.shard_map(
        for_shapes,
        mesh=mesh,
        in_specs=(P(("rep", "section"), None, "fsdp"),),
        out_specs=P(("rep", "section"), None, "fsdp"),
        check_vma=False,
    )
```

```python
import functools
import math

import jax
import jax.numpy as jnp
import numpy as np
from jax import lax
from jax.experimental import pallas as pl
from jax.experimental.pallas import tpu as pltpu
from jax.sharding import PartitionSpec as P


def tile_table(devices, band_blocks):
    block_table = np.zeros((devices, devices), dtype=np.int32)
    for row_block in range(devices):
        for col_block in range(devices):
            distance = (col_block - row_block) % devices
            if distance <= devices // 2:
                block_table[row_block, col_block] = row_block * band_blocks + distance
            else:
                block_table[row_block, col_block] = (
                    devices * band_blocks + col_block * band_blocks + (devices - distance)
                )
    return block_table


def on_device(iterate):
    devices = lax.axis_size("fsdp")
    experts, rows_all, columns = iterate.shape
    strip_rows = rows_all // devices
    band_blocks = devices // 2 + 1
    out_scale = 0.2 * math.sqrt(max(rows_all, columns * devices))
    expert_rows = iterate[0]
    row_blocks = expert_rows.reshape(devices, strip_rows, columns)

    def one_offset(offset):
        partner = jnp.roll(row_blocks, -offset, axis=0)
        tiles = jnp.einsum("nsc,ntc->nst", row_blocks, partner, preferred_element_type=jnp.float32)
        return tiles.astype(jnp.bfloat16)

    band_term = lax.map(one_offset, jnp.arange(band_blocks, dtype=jnp.int32))
    received = lax.all_to_all(band_term, "fsdp", split_axis=1, concat_axis=1, tiled=True)
    own_band = jnp.sum(received.astype(jnp.float32), axis=1).astype(jnp.bfloat16)
    upper_tiles = lax.all_gather(own_band, "fsdp", axis=0, tiled=True)
    tile_pool = jnp.concatenate([upper_tiles, jnp.swapaxes(upper_tiles, 1, 2)], axis=0)
    block_table = jnp.asarray(tile_table(devices, band_blocks))
    dense_blocks = jnp.take(tile_pool, block_table, axis=0)

    def apply_gram(operand):
        shaped = operand.reshape(devices, strip_rows, columns)
        product = jnp.einsum(
            "nmij,mjc->nic", dense_blocks, shaped, preferred_element_type=jnp.float32
        )
        return product.reshape(rows_all, columns)

    first_product = apply_gram(expert_rows)
    second_product = apply_gram(first_product.astype(jnp.bfloat16))
    combined = out_scale * (
        3.4445 * expert_rows.astype(jnp.float32) - 4.775 * first_product + 2.0315 * second_product
    )
    results = [combined.astype(jnp.bfloat16)]
    return jnp.stack(results)


CHUNK = 256
SHIFT = 4.775 / (2 * 2.0315)
BASE = 3.4445 - 4.775 * 4.775 / (4 * 2.0315)


def line_kernel(
    out_scale, chunks, direct,
    x_ref, out_ref,
    xall, gram, half, mixing, sent_rows,
    local_sem, recv_sem, inner_sem, outer_sem, mix_send, mix_recv, row_send, row_recv,
):
    me = lax.axis_index("fsdp")
    columns = x_ref.shape[1]
    width = columns * 4
    middle = jnp.logical_and(me > 0, me < 3)
    end = jnp.logical_not(middle)

    def rows_of(k):
        return pl.ds(pl.multiple_of(k * CHUNK, CHUNK), CHUNK)

    own_copy = pltpu.make_async_copy(x_ref, xall.at[me], local_sem)
    own_copy.start()

    barrier = pltpu.get_barrier_semaphore()

    @pl.when(me > 0)
    def _():
        pl.semaphore_signal(barrier, inc=1, device_id={"fsdp": me - 1}, device_id_type=pl.DeviceIdType.MESH)

    @pl.when(me < 3)
    def _():
        pl.semaphore_signal(barrier, inc=1, device_id={"fsdp": me + 1}, device_id_type=pl.DeviceIdType.MESH)

    @pl.when(middle)
    def _():
        pl.semaphore_wait(barrier, 2)

    @pl.when(end)
    def _():
        pl.semaphore_wait(barrier, 1)

    def own_chunk(k, sem, target):
        return pltpu.make_async_remote_copy(
            src_ref=x_ref.at[rows_of(k)], dst_ref=xall.at[me, rows_of(k)],
            send_sem=sem, recv_sem=recv_sem.at[me, k],
            device_id={"fsdp": target}, device_id_type=pl.DeviceIdType.MESH,
        )

    def relay_chunk(shard, k, sem, target):
        return pltpu.make_async_remote_copy(
            src_ref=xall.at[shard, rows_of(k)], dst_ref=xall.at[shard, rows_of(k)],
            send_sem=sem, recv_sem=recv_sem.at[shard, k],
            device_id={"fsdp": target}, device_id_type=pl.DeviceIdType.MESH,
        )

    def mix_copy(i, target):
        part = pl.ds(i * columns, columns)
        return pltpu.make_async_remote_copy(
            src_ref=mixing.at[0, part], dst_ref=mixing.at[0, part],
            send_sem=mix_send.at[i], recv_sem=mix_recv.at[i],
            device_id={"fsdp": target}, device_id_type=pl.DeviceIdType.MESH,
        )

    def row_copy(k, target):
        return pltpu.make_async_remote_copy(
            src_ref=sent_rows.at[pl.ds(pl.multiple_of((k - direct) * CHUNK, CHUNK), CHUNK)],
            dst_ref=out_ref.at[rows_of(k)],
            send_sem=row_send.at[k], recv_sem=row_recv.at[k],
            device_id={"fsdp": target}, device_id_type=pl.DeviceIdType.MESH,
        )

    def wide(rows):
        return jnp.concatenate([xall[q, rows, :] for q in range(4)], axis=1)

    def update_rows(shard, slot, rows):
        product = jnp.dot(wide(rows), mixing[slot], preferred_element_type=jnp.float32)
        own = xall[shard, rows, :].astype(jnp.float32)
        return (out_scale * BASE * own + product).astype(jnp.bfloat16)

    @pl.when(middle)
    def _():
        peer = 3 - me
        outer = 3 * (me - 1)
        far = 3 - outer

        @pl.loop(0, chunks)
        def _(k):
            own_chunk(k, inner_sem.at[0, k], peer).start()

            @pl.when(k < direct)
            def _():
                own_chunk(k, outer_sem.at[0, k], outer).start()

        for i in range(4):
            row_ids = lax.broadcasted_iota(jnp.int32, (columns, width), 0) + i * columns
            column_ids = lax.broadcasted_iota(jnp.int32, (columns, width), 1)
            start = jnp.where(row_ids == column_ids, jnp.float32(-SHIFT), jnp.float32(0))
            for j in range(4):
                gram[i, j] = start[:, j * columns:(j + 1) * columns]
        own_copy.wait()

        @pl.loop(0, chunks)
        def _(k):
            relay_chunk(outer, k, inner_sem.at[1, k], peer).wait_recv()
            relay_chunk(outer, k, inner_sem.at[1, k], peer).start()
            relay_chunk(peer, k, outer_sem.at[1, k], outer).wait_recv()

            @pl.when(k < direct)
            def _():
                relay_chunk(peer, k, outer_sem.at[1, k], outer).start()

        def take_far(k):
            relay_chunk(far, k, outer_sem.at[2, k], outer).wait_recv()

            @pl.when(k < direct)
            def _():
                relay_chunk(far, k, outer_sem.at[2, k], outer).start()

        def turned(left, right):
            return lax.dot_general(
                left, right, (((0,), (0,)), ((), ())), preferred_element_type=jnp.float32
            )

        @pl.loop(0, chunks - 1)
        def _(k):
            take_far(k)
            for i in range(4):
                product = turned(xall[i, rows_of(k), :], wide(rows_of(k)))
                for j in range(4):
                    gram[i, j] += product[:, j * columns:(j + 1) * columns]

        last = rows_of(chunks - 1)

        def finish(i, j):
            total = gram[i, j] + turned(xall[i, last, :], xall[j, last, :])
            half[j, pl.ds(pl.multiple_of(i * columns, columns), columns), :] = total.astype(jnp.bfloat16)

        near = (me, peer, outer)
        for i in near:
            for j in near:
                finish(i, j)
        take_far(chunks - 1)
        for i in near:
            finish(far, i)
            finish(i, far)
        finish(far, far)

        def mix(slot, shard, send):
            for i in range(4):
                left = jnp.concatenate(
                    [half[j, i * columns:(i + 1) * columns, :] for j in range(4)], axis=1
                )
                square = jnp.dot(left, half[shard], preferred_element_type=jnp.float32)
                mixing[slot, i * columns:(i + 1) * columns, :] = (
                    (out_scale * 2.0315) * square
                ).astype(jnp.bfloat16)
                if send:
                    mix_copy(i, outer).start()

        mix(0, outer, True)

        @pl.loop(direct, chunks)
        def _(k):
            sent_rows[pl.ds(pl.multiple_of((k - direct) * CHUNK, CHUNK), CHUNK), :] = update_rows(
                outer, 0, rows_of(k)
            )
            row_copy(k, outer).start()

        mix(1, me, False)

        @pl.loop(0, chunks)
        def _(k):
            out_ref[rows_of(k), :] = update_rows(me, 1, rows_of(k))

        @pl.loop(0, chunks)
        def _(k):
            own_chunk(k, inner_sem.at[0, k], peer).wait_send()
            relay_chunk(outer, k, inner_sem.at[1, k], peer).wait_send()

        @pl.loop(0, direct)
        def _(k):
            own_chunk(k, outer_sem.at[0, k], outer).wait_send()
            relay_chunk(peer, k, outer_sem.at[1, k], outer).wait_send()
            relay_chunk(far, k, outer_sem.at[2, k], outer).wait_send()

        for i in range(4):
            mix_copy(i, outer).wait_send()

        @pl.loop(direct, chunks)
        def _(k):
            row_copy(k, outer).wait_send()

    @pl.when(end)
    def _():
        inner = 1 + me // 3

        @pl.loop(0, chunks)
        def _(k):
            own_chunk(k, inner_sem.at[0, k], inner).start()

        own_copy.wait()
        for hop in range(3):
            shard = inner + hop * (1 - 2 * (me // 3))

            @pl.loop(0, direct)
            def _(k):
                relay_chunk(shard, k, outer_sem.at[0, k], inner).wait_recv()

        for i in range(4):
            mix_copy(i, inner).wait_recv()

        @pl.loop(0, direct)
        def _(k):
            out_ref[rows_of(k), :] = update_rows(me, 0, rows_of(k))

        @pl.loop(0, chunks)
        def _(k):
            own_chunk(k, inner_sem.at[0, k], inner).wait_send()

        @pl.loop(direct, chunks)
        def _(k):
            row_copy(k, inner).wait_recv()


def on_device_line(iterate):
    _, rows_all, columns = iterate.shape
    width = columns * 4
    chunks = rows_all // CHUNK
    direct = 2 * chunks // 3
    out_scale = 0.2 * math.sqrt(max(rows_all, width))
    update = pl.pallas_call(
        functools.partial(line_kernel, out_scale, chunks, direct),
        out_shape=pltpu.VMEM((rows_all, columns), jnp.bfloat16),
        in_specs=[pl.BlockSpec(memory_space=pltpu.HBM)],
        out_specs=pl.BlockSpec(memory_space=pltpu.VMEM),
        scratch_shapes=[
            pltpu.VMEM((4, rows_all, columns), jnp.bfloat16),
            pltpu.VMEM((4, 4, columns, columns), jnp.float32),
            pltpu.VMEM((4, width, columns), jnp.bfloat16),
            pltpu.VMEM((2, width, columns), jnp.bfloat16),
            pltpu.VMEM(((chunks - direct) * CHUNK, columns), jnp.bfloat16),
            pltpu.SemaphoreType.DMA,
            pltpu.SemaphoreType.DMA((4, chunks)),
            pltpu.SemaphoreType.DMA((2, chunks)),
            pltpu.SemaphoreType.DMA((3, chunks)),
            pltpu.SemaphoreType.DMA((4,)),
            pltpu.SemaphoreType.DMA((4,)),
            pltpu.SemaphoreType.DMA((chunks,)),
            pltpu.SemaphoreType.DMA((chunks,)),
        ],
        compiler_params=pltpu.CompilerParams(
            collective_id=0, has_side_effects=True, vmem_limit_bytes=40 << 20
        ),
    )(pltpu.with_memory_space_constraint(iterate[0], pltpu.HBM))
    return update[None]


def for_shapes(iterate):
    _, rows_all, columns = iterate.shape
    devices = lax.axis_size("fsdp")
    fits = columns % 256 == 0 and rows_all % (3 * CHUNK) == 0
    if devices == 4 and columns * devices <= rows_all and fits:
        return on_device_line(iterate)
    return on_device(iterate)


def solution(mesh):
    return jax.shard_map(
        for_shapes,
        mesh=mesh,
        in_specs=(P(("rep", "section"), None, "fsdp"),),
        out_specs=P(("rep", "section"), None, "fsdp"),
        check_vma=False,
    )
```

```python
import functools
import math

import jax
import jax.numpy as jnp
import numpy as np
from jax import lax
from jax.experimental import pallas as pl
from jax.experimental.pallas import tpu as pltpu
from jax.sharding import PartitionSpec as P


def tile_table(devices, band_blocks):
    block_table = np.zeros((devices, devices), dtype=np.int32)
    for row_block in range(devices):
        for col_block in range(devices):
            distance = (col_block - row_block) % devices
            if distance <= devices // 2:
                block_table[row_block, col_block] = row_block * band_blocks + distance
            else:
                block_table[row_block, col_block] = (
                    devices * band_blocks + col_block * band_blocks + (devices - distance)
                )
    return block_table


def on_device(iterate):
    devices = lax.axis_size("fsdp")
    experts, rows_all, columns = iterate.shape
    strip_rows = rows_all // devices
    band_blocks = devices // 2 + 1
    out_scale = 0.2 * math.sqrt(max(rows_all, columns * devices))
    expert_rows = iterate[0]
    row_blocks = expert_rows.reshape(devices, strip_rows, columns)

    def one_offset(offset):
        partner = jnp.roll(row_blocks, -offset, axis=0)
        tiles = jnp.einsum("nsc,ntc->nst", row_blocks, partner, preferred_element_type=jnp.float32)
        return tiles.astype(jnp.bfloat16)

    band_term = lax.map(one_offset, jnp.arange(band_blocks, dtype=jnp.int32))
    received = lax.all_to_all(band_term, "fsdp", split_axis=1, concat_axis=1, tiled=True)
    own_band = jnp.sum(received.astype(jnp.float32), axis=1).astype(jnp.bfloat16)
    upper_tiles = lax.all_gather(own_band, "fsdp", axis=0, tiled=True)
    tile_pool = jnp.concatenate([upper_tiles, jnp.swapaxes(upper_tiles, 1, 2)], axis=0)
    block_table = jnp.asarray(tile_table(devices, band_blocks))
    dense_blocks = jnp.take(tile_pool, block_table, axis=0)

    def apply_gram(operand):
        shaped = operand.reshape(devices, strip_rows, columns)
        product = jnp.einsum(
            "nmij,mjc->nic", dense_blocks, shaped, preferred_element_type=jnp.float32
        )
        return product.reshape(rows_all, columns)

    first_product = apply_gram(expert_rows)
    second_product = apply_gram(first_product.astype(jnp.bfloat16))
    combined = out_scale * (
        3.4445 * expert_rows.astype(jnp.float32) - 4.775 * first_product + 2.0315 * second_product
    )
    results = [combined.astype(jnp.bfloat16)]
    return jnp.stack(results)


CHUNK = 512
FILL = 64
SHIFT = 4.775 / (2 * 2.0315)
BASE = 3.4445 - 4.775 * 4.775 / (4 * 2.0315)


def line_kernel(
    out_scale, chunks, direct,
    x_ref, out_ref,
    xall, gram, half, mixing, sent_rows,
    local_sem, recv_sem, fill_send, fill_recv, inner_sem, outer_sem, mix_send, mix_recv, row_send, row_recv,
):
    me = lax.axis_index("fsdp")
    columns = x_ref.shape[1]
    width = columns * 4
    middle = jnp.logical_and(me > 0, me < 3)
    end = jnp.logical_not(middle)

    def rows_of(k):
        return pl.ds(pl.multiple_of(k * CHUNK, CHUNK), CHUNK)

    own_copy = pltpu.make_async_copy(x_ref, xall.at[me], local_sem)
    own_copy.start()

    barrier = pltpu.get_barrier_semaphore()

    @pl.when(me > 0)
    def _():
        pl.semaphore_signal(barrier, inc=1, device_id={"fsdp": me - 1}, device_id_type=pl.DeviceIdType.MESH)

    @pl.when(me < 3)
    def _():
        pl.semaphore_signal(barrier, inc=1, device_id={"fsdp": me + 1}, device_id_type=pl.DeviceIdType.MESH)

    @pl.when(middle)
    def _():
        pl.semaphore_wait(barrier, 2)

    @pl.when(end)
    def _():
        pl.semaphore_wait(barrier, 1)

    def own_chunk(k, sem, target):
        return pltpu.make_async_remote_copy(
            src_ref=x_ref.at[rows_of(k)], dst_ref=xall.at[me, rows_of(k)],
            send_sem=sem, recv_sem=recv_sem.at[me, k],
            device_id={"fsdp": target}, device_id_type=pl.DeviceIdType.MESH,
        )

    def relay_chunk(shard, k, sem, target):
        return pltpu.make_async_remote_copy(
            src_ref=xall.at[shard, rows_of(k)], dst_ref=xall.at[shard, rows_of(k)],
            send_sem=sem, recv_sem=recv_sem.at[shard, k],
            device_id={"fsdp": target}, device_id_type=pl.DeviceIdType.MESH,
        )

    fill = pl.ds(direct * CHUNK, FILL)
    rest = pl.ds(direct * CHUNK + FILL, CHUNK - FILL)

    def fill_copy(shard, source, sem, target):
        return pltpu.make_async_remote_copy(
            src_ref=source, dst_ref=xall.at[shard, fill],
            send_sem=fill_send.at[sem], recv_sem=fill_recv.at[shard],
            device_id={"fsdp": target}, device_id_type=pl.DeviceIdType.MESH,
        )

    def rest_copy(target):
        return pltpu.make_async_remote_copy(
            src_ref=sent_rows.at[pl.ds(FILL, CHUNK - FILL)], dst_ref=out_ref.at[rest],
            send_sem=row_send.at[direct], recv_sem=row_recv.at[direct],
            device_id={"fsdp": target}, device_id_type=pl.DeviceIdType.MESH,
        )

    def mix_copy(i, target):
        part = pl.ds(i * columns, columns)
        return pltpu.make_async_remote_copy(
            src_ref=mixing.at[0, part], dst_ref=mixing.at[0, part],
            send_sem=mix_send.at[i], recv_sem=mix_recv.at[i],
            device_id={"fsdp": target}, device_id_type=pl.DeviceIdType.MESH,
        )

    def row_copy(k, target):
        return pltpu.make_async_remote_copy(
            src_ref=sent_rows.at[pl.ds(pl.multiple_of((k - direct) * CHUNK, CHUNK), CHUNK)],
            dst_ref=out_ref.at[rows_of(k)],
            send_sem=row_send.at[k], recv_sem=row_recv.at[k],
            device_id={"fsdp": target}, device_id_type=pl.DeviceIdType.MESH,
        )

    def wide(rows):
        return jnp.concatenate([xall[q, rows, :] for q in range(4)], axis=1)

    def update_rows(shard, slot, rows):
        product = jnp.dot(wide(rows), mixing[slot], preferred_element_type=jnp.float32)
        own = xall[shard, rows, :].astype(jnp.float32)
        return (out_scale * BASE * own + product).astype(jnp.bfloat16)

    @pl.when(middle)
    def _():
        peer = 3 - me
        outer = 3 * (me - 1)
        far = 3 - outer

        @pl.loop(0, chunks)
        def _(k):
            own_chunk(k, inner_sem.at[0, k], peer).start()

            @pl.when(k < direct)
            def _():
                own_chunk(k, outer_sem.at[0, k], outer).start()

        fill_copy(me, x_ref.at[fill], 0, outer).start()

        for i in range(4):
            row_ids = lax.broadcasted_iota(jnp.int32, (columns, width), 0) + i * columns
            column_ids = lax.broadcasted_iota(jnp.int32, (columns, width), 1)
            start = jnp.where(row_ids == column_ids, jnp.float32(-SHIFT), jnp.float32(0))
            for j in range(4):
                gram[i, j] = start[:, j * columns:(j + 1) * columns]
        own_copy.wait()

        @pl.loop(0, chunks)
        def _(k):
            relay_chunk(outer, k, inner_sem.at[1, k], peer).wait_recv()
            relay_chunk(outer, k, inner_sem.at[1, k], peer).start()
            relay_chunk(peer, k, outer_sem.at[1, k], outer).wait_recv()

            @pl.when(k < direct)
            def _():
                relay_chunk(peer, k, outer_sem.at[1, k], outer).start()

            @pl.when(k == direct)
            def _():
                fill_copy(peer, xall.at[peer, fill], 1, outer).start()

        def take_far(k):
            relay_chunk(far, k, outer_sem.at[2, k], outer).wait_recv()

            @pl.when(k < direct)
            def _():
                relay_chunk(far, k, outer_sem.at[2, k], outer).start()

        def turned(left, right):
            return lax.dot_general(
                left, right, (((0,), (0,)), ((), ())), preferred_element_type=jnp.float32
            )

        @pl.loop(0, chunks - 1)
        def _(k):
            take_far(k)

            @pl.when(k == direct)
            def _():
                fill_copy(far, xall.at[far, fill], 2, outer).start()

            for i in range(4):
                product = turned(xall[i, rows_of(k), :], wide(rows_of(k)))
                for j in range(4):
                    gram[i, j] += product[:, j * columns:(j + 1) * columns]

        last = rows_of(chunks - 1)

        def finish(i, j):
            total = gram[i, j] + turned(xall[i, last, :], xall[j, last, :])
            half[j, pl.ds(pl.multiple_of(i * columns, columns), columns), :] = total.astype(jnp.bfloat16)

        near = (me, peer, outer)
        for i in near:
            for j in near:
                finish(i, j)
        take_far(chunks - 1)
        for i in near:
            finish(far, i)
            finish(i, far)
        finish(far, far)

        def mix(slot, shard, send):
            for i in range(4):
                left = jnp.concatenate(
                    [half[j, i * columns:(i + 1) * columns, :] for j in range(4)], axis=1
                )
                square = jnp.dot(left, half[shard], preferred_element_type=jnp.float32)
                mixing[slot, i * columns:(i + 1) * columns, :] = (
                    (out_scale * 2.0315) * square
                ).astype(jnp.bfloat16)
                if send:
                    mix_copy(i, outer).start()

        mix(0, outer, True)

        sent_rows[FILL:CHUNK, :] = update_rows(outer, 0, rest)
        rest_copy(outer).start()

        @pl.loop(direct + 1, chunks)
        def _(k):
            sent_rows[pl.ds(pl.multiple_of((k - direct) * CHUNK, CHUNK), CHUNK), :] = update_rows(
                outer, 0, rows_of(k)
            )
            row_copy(k, outer).start()

        mix(1, me, False)

        @pl.loop(0, chunks)
        def _(k):
            out_ref[rows_of(k), :] = update_rows(me, 1, rows_of(k))

        @pl.loop(0, chunks)
        def _(k):
            own_chunk(k, inner_sem.at[0, k], peer).wait_send()
            relay_chunk(outer, k, inner_sem.at[1, k], peer).wait_send()

        @pl.loop(0, direct)
        def _(k):
            own_chunk(k, outer_sem.at[0, k], outer).wait_send()
            relay_chunk(peer, k, outer_sem.at[1, k], outer).wait_send()
            relay_chunk(far, k, outer_sem.at[2, k], outer).wait_send()

        for i in range(4):
            mix_copy(i, outer).wait_send()

        fill_copy(me, x_ref.at[fill], 0, outer).wait_send()
        fill_copy(peer, xall.at[peer, fill], 1, outer).wait_send()
        fill_copy(far, xall.at[far, fill], 2, outer).wait_send()
        rest_copy(outer).wait_send()

        @pl.loop(direct + 1, chunks)
        def _(k):
            row_copy(k, outer).wait_send()

    @pl.when(end)
    def _():
        inner = 1 + me // 3

        @pl.loop(0, chunks)
        def _(k):
            own_chunk(k, inner_sem.at[0, k], inner).start()

        own_copy.wait()
        for hop in range(3):
            shard = inner + hop * (1 - 2 * (me // 3))

            @pl.loop(0, direct)
            def _(k):
                relay_chunk(shard, k, outer_sem.at[0, k], inner).wait_recv()

            fill_copy(shard, xall.at[shard, fill], 0, inner).wait_recv()

        for i in range(4):
            mix_copy(i, inner).wait_recv()

        @pl.loop(0, direct)
        def _(k):
            out_ref[rows_of(k), :] = update_rows(me, 0, rows_of(k))

        out_ref[fill, :] = update_rows(me, 0, fill)

        @pl.loop(0, chunks)
        def _(k):
            own_chunk(k, inner_sem.at[0, k], inner).wait_send()

        rest_copy(inner).wait_recv()

        @pl.loop(direct + 1, chunks)
        def _(k):
            row_copy(k, inner).wait_recv()


def on_device_line(iterate):
    _, rows_all, columns = iterate.shape
    width = columns * 4
    chunks = rows_all // CHUNK
    direct = 2 * chunks // 3
    out_scale = 0.2 * math.sqrt(max(rows_all, width))
    update = pl.pallas_call(
        functools.partial(line_kernel, out_scale, chunks, direct),
        out_shape=pltpu.VMEM((rows_all, columns), jnp.bfloat16),
        in_specs=[pl.BlockSpec(memory_space=pltpu.HBM)],
        out_specs=pl.BlockSpec(memory_space=pltpu.VMEM),
        scratch_shapes=[
            pltpu.VMEM((4, rows_all, columns), jnp.bfloat16),
            pltpu.VMEM((4, 4, columns, columns), jnp.float32),
            pltpu.VMEM((4, width, columns), jnp.bfloat16),
            pltpu.VMEM((2, width, columns), jnp.bfloat16),
            pltpu.VMEM(((chunks - direct) * CHUNK, columns), jnp.bfloat16),
            pltpu.SemaphoreType.DMA,
            pltpu.SemaphoreType.DMA((4, chunks)),
            pltpu.SemaphoreType.DMA((3,)),
            pltpu.SemaphoreType.DMA((4,)),
            pltpu.SemaphoreType.DMA((2, chunks)),
            pltpu.SemaphoreType.DMA((3, chunks)),
            pltpu.SemaphoreType.DMA((4,)),
            pltpu.SemaphoreType.DMA((4,)),
            pltpu.SemaphoreType.DMA((chunks,)),
            pltpu.SemaphoreType.DMA((chunks,)),
        ],
        compiler_params=pltpu.CompilerParams(
            collective_id=0, has_side_effects=True, vmem_limit_bytes=40 << 20
        ),
    )(pltpu.with_memory_space_constraint(iterate[0], pltpu.HBM))
    return update[None]


def for_shapes(iterate):
    _, rows_all, columns = iterate.shape
    devices = lax.axis_size("fsdp")
    fits = columns % 256 == 0 and rows_all % (3 * CHUNK) == 0
    if devices == 4 and columns * devices <= rows_all and fits:
        return on_device_line(iterate)
    return on_device(iterate)


def solution(mesh):
    return jax.shard_map(
        for_shapes,
        mesh=mesh,
        in_specs=(P(("rep", "section"), None, "fsdp"),),
        out_specs=P(("rep", "section"), None, "fsdp"),
        check_vma=False,
    )
```

```python
import functools
import math

import jax
import jax.numpy as jnp
import numpy as np
from jax import lax
from jax.experimental import pallas as pl
from jax.experimental.pallas import tpu as pltpu
from jax.sharding import PartitionSpec as P


def tile_table(devices, band_blocks):
    block_table = np.zeros((devices, devices), dtype=np.int32)
    for row_block in range(devices):
        for col_block in range(devices):
            distance = (col_block - row_block) % devices
            if distance <= devices // 2:
                block_table[row_block, col_block] = row_block * band_blocks + distance
            else:
                block_table[row_block, col_block] = (
                    devices * band_blocks + col_block * band_blocks + (devices - distance)
                )
    return block_table


def on_device(iterate):
    devices = lax.axis_size("fsdp")
    experts, rows_all, columns = iterate.shape
    strip_rows = rows_all // devices
    band_blocks = devices // 2 + 1
    out_scale = 0.2 * math.sqrt(max(rows_all, columns * devices))
    expert_rows = iterate[0]
    row_blocks = expert_rows.reshape(devices, strip_rows, columns)

    def one_offset(offset):
        partner = jnp.roll(row_blocks, -offset, axis=0)
        tiles = jnp.einsum("nsc,ntc->nst", row_blocks, partner, preferred_element_type=jnp.float32)
        return tiles.astype(jnp.bfloat16)

    band_term = lax.map(one_offset, jnp.arange(band_blocks, dtype=jnp.int32))
    received = lax.all_to_all(band_term, "fsdp", split_axis=1, concat_axis=1, tiled=True)
    own_band = jnp.sum(received.astype(jnp.float32), axis=1).astype(jnp.bfloat16)
    upper_tiles = lax.all_gather(own_band, "fsdp", axis=0, tiled=True)
    tile_pool = jnp.concatenate([upper_tiles, jnp.swapaxes(upper_tiles, 1, 2)], axis=0)
    block_table = jnp.asarray(tile_table(devices, band_blocks))
    dense_blocks = jnp.take(tile_pool, block_table, axis=0)

    def apply_gram(operand):
        shaped = operand.reshape(devices, strip_rows, columns)
        product = jnp.einsum(
            "nmij,mjc->nic", dense_blocks, shaped, preferred_element_type=jnp.float32
        )
        return product.reshape(rows_all, columns)

    first_product = apply_gram(expert_rows)
    second_product = apply_gram(first_product.astype(jnp.bfloat16))
    combined = out_scale * (
        3.4445 * expert_rows.astype(jnp.float32) - 4.775 * first_product + 2.0315 * second_product
    )
    results = [combined.astype(jnp.bfloat16)]
    return jnp.stack(results)


CHUNK = 512
FILL = 64
SHIFT = 4.775 / (2 * 2.0315)
BASE = 3.4445 - 4.775 * 4.775 / (4 * 2.0315)


def line_kernel(
    out_scale, chunks, direct,
    x_ref, out_ref,
    xall, gram, half, mixing, sent_rows,
    local_sem, recv_sem, fill_send, fill_recv, inner_sem, outer_sem, mix_send, mix_recv, row_send, row_recv,
):
    me = lax.axis_index("fsdp")
    columns = x_ref.shape[1]
    width = columns * 4
    middle = jnp.logical_and(me > 0, me < 3)
    end = jnp.logical_not(middle)

    def rows_of(k):
        return pl.ds(pl.multiple_of(k * CHUNK, CHUNK), CHUNK)

    own_copy = pltpu.make_async_copy(x_ref, xall.at[me], local_sem)
    own_copy.start()

    barrier = pltpu.get_barrier_semaphore()

    @pl.when(me > 0)
    def _():
        pl.semaphore_signal(barrier, inc=1, device_id={"fsdp": me - 1}, device_id_type=pl.DeviceIdType.MESH)

    @pl.when(me < 3)
    def _():
        pl.semaphore_signal(barrier, inc=1, device_id={"fsdp": me + 1}, device_id_type=pl.DeviceIdType.MESH)

    @pl.when(middle)
    def _():
        pl.semaphore_wait(barrier, 2)

    @pl.when(end)
    def _():
        pl.semaphore_wait(barrier, 1)

    def own_chunk(k, sem, target):
        return pltpu.make_async_remote_copy(
            src_ref=x_ref.at[rows_of(k)], dst_ref=xall.at[me, rows_of(k)],
            send_sem=sem, recv_sem=recv_sem.at[me, k],
            device_id={"fsdp": target}, device_id_type=pl.DeviceIdType.MESH,
        )

    def relay_chunk(shard, k, sem, target):
        return pltpu.make_async_remote_copy(
            src_ref=xall.at[shard, rows_of(k)], dst_ref=xall.at[shard, rows_of(k)],
            send_sem=sem, recv_sem=recv_sem.at[shard, k],
            device_id={"fsdp": target}, device_id_type=pl.DeviceIdType.MESH,
        )

    fill = pl.ds(direct * CHUNK, FILL)
    rest = pl.ds(direct * CHUNK + FILL, CHUNK - FILL)

    def fill_copy(shard, source, sem, target):
        return pltpu.make_async_remote_copy(
            src_ref=source, dst_ref=xall.at[shard, fill],
            send_sem=fill_send.at[sem], recv_sem=fill_recv.at[shard],
            device_id={"fsdp": target}, device_id_type=pl.DeviceIdType.MESH,
        )

    def rest_copy(target):
        return pltpu.make_async_remote_copy(
            src_ref=sent_rows.at[pl.ds(FILL, CHUNK - FILL)], dst_ref=out_ref.at[rest],
            send_sem=row_send.at[direct], recv_sem=row_recv.at[direct],
            device_id={"fsdp": target}, device_id_type=pl.DeviceIdType.MESH,
        )

    def mix_copy(i, target):
        part = pl.ds(i * columns, columns)
        return pltpu.make_async_remote_copy(
            src_ref=mixing.at[0, part], dst_ref=mixing.at[0, part],
            send_sem=mix_send.at[i], recv_sem=mix_recv.at[i],
            device_id={"fsdp": target}, device_id_type=pl.DeviceIdType.MESH,
        )

    def row_copy(k, target):
        return pltpu.make_async_remote_copy(
            src_ref=sent_rows.at[pl.ds(pl.multiple_of((k - direct) * CHUNK, CHUNK), CHUNK)],
            dst_ref=out_ref.at[rows_of(k)],
            send_sem=row_send.at[k], recv_sem=row_recv.at[k],
            device_id={"fsdp": target}, device_id_type=pl.DeviceIdType.MESH,
        )

    def wide(rows):
        return jnp.concatenate([xall[q, rows, :] for q in range(4)], axis=1)

    def update_rows(shard, slot, rows):
        product = jnp.dot(wide(rows), mixing[slot], preferred_element_type=jnp.float32)
        own = xall[shard, rows, :].astype(jnp.float32)
        return (out_scale * BASE * own + product).astype(jnp.bfloat16)

    @pl.when(middle)
    def _():
        peer = 3 - me
        outer = 3 * (me - 1)
        far = 3 - outer

        @pl.loop(0, chunks)
        def _(k):
            own_chunk(k, inner_sem.at[0, k], peer).start()

            @pl.when(k < direct)
            def _():
                own_chunk(k, outer_sem.at[0, k], outer).start()

        fill_copy(me, x_ref.at[fill], 0, outer).start()

        for i in range(4):
            row_ids = lax.broadcasted_iota(jnp.int32, (columns, width), 0) + i * columns
            column_ids = lax.broadcasted_iota(jnp.int32, (columns, width), 1)
            start = jnp.where(row_ids == column_ids, jnp.float32(-SHIFT), jnp.float32(0))
            for j in range(4):
                gram[i, j] = start[:, j * columns:(j + 1) * columns]
        own_copy.wait()

        @pl.loop(0, chunks)
        def _(k):
            relay_chunk(outer, k, inner_sem.at[1, k], peer).wait_recv()
            relay_chunk(outer, k, inner_sem.at[1, k], peer).start()
            relay_chunk(peer, k, outer_sem.at[1, k], outer).wait_recv()

            @pl.when(k < direct)
            def _():
                relay_chunk(peer, k, outer_sem.at[1, k], outer).start()

            @pl.when(k == direct)
            def _():
                fill_copy(peer, xall.at[peer, fill], 1, outer).start()

        def take_far(k):
            relay_chunk(far, k, outer_sem.at[2, k], outer).wait_recv()

            @pl.when(k < direct)
            def _():
                relay_chunk(far, k, outer_sem.at[2, k], outer).start()

        def turned(left, right):
            return lax.dot_general(
                left, right, (((0,), (0,)), ((), ())), preferred_element_type=jnp.float32
            )

        @pl.loop(0, chunks - 1)
        def _(k):
            take_far(k)

            @pl.when(k == direct)
            def _():
                fill_copy(far, xall.at[far, fill], 2, outer).start()

            for i in range(4):
                product = turned(xall[i, rows_of(k), :], wide(rows_of(k)))
                for j in range(4):
                    gram[i, j] += product[:, j * columns:(j + 1) * columns]

        last = rows_of(chunks - 1)

        def finish(i, j):
            total = gram[i, j] + turned(xall[i, last, :], xall[j, last, :])
            half[j, pl.ds(pl.multiple_of(i * columns, columns), columns), :] = total.astype(jnp.bfloat16)

        near = (me, peer, outer)
        for i in near:
            for j in near:
                finish(i, j)
        take_far(chunks - 1)
        for i in near:
            finish(far, i)
            finish(i, far)
        finish(far, far)

        def mix(slot, shard, send):
            for i in range(4):
                left = jnp.concatenate(
                    [half[j, i * columns:(i + 1) * columns, :] for j in range(4)], axis=1
                )
                square = jnp.dot(left, half[shard], preferred_element_type=jnp.float32)
                mixing[slot, i * columns:(i + 1) * columns, :] = (
                    (out_scale * 2.0315) * square
                ).astype(jnp.bfloat16)
                if send:
                    mix_copy(i, outer).start()

        mix(0, outer, True)

        sent_rows[FILL:CHUNK, :] = update_rows(outer, 0, rest)
        rest_copy(outer).start()

        @pl.loop(direct + 1, chunks)
        def _(k):
            sent_rows[pl.ds(pl.multiple_of((k - direct) * CHUNK, CHUNK), CHUNK), :] = update_rows(
                outer, 0, rows_of(k)
            )
            row_copy(k, outer).start()

        mix(1, me, False)

        @pl.loop(0, chunks)
        def _(k):
            out_ref[rows_of(k), :] = update_rows(me, 1, rows_of(k))

        @pl.loop(0, chunks)
        def _(k):
            own_chunk(k, inner_sem.at[0, k], peer).wait_send()
            relay_chunk(outer, k, inner_sem.at[1, k], peer).wait_send()

        @pl.loop(0, direct)
        def _(k):
            own_chunk(k, outer_sem.at[0, k], outer).wait_send()
            relay_chunk(peer, k, outer_sem.at[1, k], outer).wait_send()
            relay_chunk(far, k, outer_sem.at[2, k], outer).wait_send()

        for i in range(4):
            mix_copy(i, outer).wait_send()

        fill_copy(me, x_ref.at[fill], 0, outer).wait_send()
        fill_copy(peer, xall.at[peer, fill], 1, outer).wait_send()
        fill_copy(far, xall.at[far, fill], 2, outer).wait_send()
        rest_copy(outer).wait_send()

        @pl.loop(direct + 1, chunks)
        def _(k):
            row_copy(k, outer).wait_send()

    @pl.when(end)
    def _():
        inner = 1 + me // 3

        @pl.loop(0, chunks)
        def _(k):
            own_chunk(k, inner_sem.at[0, k], inner).start()

        own_copy.wait()
        for hop in range(3):
            shard = inner + hop * (1 - 2 * (me // 3))

            @pl.loop(0, direct)
            def _(k):
                relay_chunk(shard, k, outer_sem.at[0, k], inner).wait_recv()

            fill_copy(shard, xall.at[shard, fill], 0, inner).wait_recv()

        for i in range(4):
            mix_copy(i, inner).wait_recv()

        @pl.loop(0, direct)
        def _(k):
            out_ref[rows_of(k), :] = update_rows(me, 0, rows_of(k))

        out_ref[fill, :] = update_rows(me, 0, fill)

        @pl.loop(0, chunks)
        def _(k):
            own_chunk(k, inner_sem.at[0, k], inner).wait_send()

        rest_copy(inner).wait_recv()

        @pl.loop(direct + 1, chunks)
        def _(k):
            row_copy(k, inner).wait_recv()


def write_out(update_ref, out_ref, sems):
    pieces = sems.shape[0]
    rows = out_ref.shape[0] // pieces
    copies = [
        pltpu.make_async_copy(
            update_ref.at[pl.ds(i * rows, rows)], out_ref.at[pl.ds(i * rows, rows)], sems.at[i]
        )
        for i in range(pieces)
    ]
    for copy in copies:
        copy.start()
    for copy in copies:
        copy.wait()


def on_device_line(iterate):
    _, rows_all, columns = iterate.shape
    width = columns * 4
    chunks = rows_all // CHUNK
    direct = 2 * chunks // 3
    out_scale = 0.2 * math.sqrt(max(rows_all, width))
    update = pl.pallas_call(
        functools.partial(line_kernel, out_scale, chunks, direct),
        out_shape=pltpu.VMEM((rows_all, columns), jnp.bfloat16),
        in_specs=[pl.BlockSpec(memory_space=pltpu.HBM)],
        out_specs=pl.BlockSpec(memory_space=pltpu.VMEM),
        scratch_shapes=[
            pltpu.VMEM((4, rows_all, columns), jnp.bfloat16),
            pltpu.VMEM((4, 4, columns, columns), jnp.float32),
            pltpu.VMEM((4, width, columns), jnp.bfloat16),
            pltpu.VMEM((2, width, columns), jnp.bfloat16),
            pltpu.VMEM(((chunks - direct) * CHUNK, columns), jnp.bfloat16),
            pltpu.SemaphoreType.DMA,
            pltpu.SemaphoreType.DMA((4, chunks)),
            pltpu.SemaphoreType.DMA((3,)),
            pltpu.SemaphoreType.DMA((4,)),
            pltpu.SemaphoreType.DMA((2, chunks)),
            pltpu.SemaphoreType.DMA((3, chunks)),
            pltpu.SemaphoreType.DMA((4,)),
            pltpu.SemaphoreType.DMA((4,)),
            pltpu.SemaphoreType.DMA((chunks,)),
            pltpu.SemaphoreType.DMA((chunks,)),
        ],
        compiler_params=pltpu.CompilerParams(
            collective_id=0, has_side_effects=True, vmem_limit_bytes=40 << 20
        ),
    )(pltpu.with_memory_space_constraint(iterate[0], pltpu.HBM))
    written = pl.pallas_call(
        write_out,
        out_shape=jax.ShapeDtypeStruct((rows_all, columns), jnp.bfloat16),
        in_specs=[pl.BlockSpec(memory_space=pltpu.VMEM)],
        out_specs=pl.BlockSpec(memory_space=pl.ANY),
        scratch_shapes=[pltpu.SemaphoreType.DMA((8,))],
    )(pltpu.with_memory_space_constraint(update, pltpu.VMEM))
    return written[None]


def for_shapes(iterate):
    _, rows_all, columns = iterate.shape
    devices = lax.axis_size("fsdp")
    fits = columns % 256 == 0 and rows_all % (3 * CHUNK) == 0
    if devices == 4 and columns * devices <= rows_all and fits:
        return on_device_line(iterate)
    return on_device(iterate)


def solution(mesh):
    return jax.shard_map(
        for_shapes,
        mesh=mesh,
        in_specs=(P(("rep", "section"), None, "fsdp"),),
        out_specs=P(("rep", "section"), None, "fsdp"),
        check_vma=False,
    )
```
